32 devices in a mesh: tm: 8 (over y, x, core), space: 4 (over z).
Axes of the slice: x: 2, y: 2, z: 4, core: 2. Of those that a mesh axis runs over, the one named last changes fastest.
Arguments:
- slice_start: float32 [8, 64, 512], P('tm', None, 'space'), may hold values from -6 to 6
- conductance: float32 [64, 512], P(None, 'space'), may hold values from 0.5 to 2
- excitation: float32 [8, 2, 64, 512], P('tm', None, None, 'space'), may hold values from -6 to 6
- self_blocks: float32 [64, 64, 512], P(None, None, 'space')
- coupling: bfloat16 [6, 64, 64, 512], P(None, None, None, 'space'), may hold values from -0.59765625 to 0.59765625
- neighbour_cols: int32 [6, 512], P(None, 'space'), may hold values from 0 to 511, as said below
- mortar: bfloat16 [64, 64, 256], P(None, None, 'space'), may hold values from -0.59765625 to 0.59765625
- inverse_blocks: float32 [64, 64, 512], P(None, None, 'space')
- offsets: int32 [8], P('tm'), may hold values from 0 to 255
Outputs:
- new_start: float32 [8, 64, 512], P('tm', None, 'space')
- correction: float32 [8, 64, 512], P('tm', None, 'space')
The draws below stay inside these ranges and needn't reach their ends.
Inputs may be any that keep to these rules, and one draw needn't show every extreme that they name: `neighbour_cols`: every neighbour block lies within 32 blocks of its row along the closed azimuthal order (index modulo 512) and is never the row itself; in every draw some rows reach exactly 32 on each side.
All inputs are finite; a program needn't handle non-finite values.
Results may differ from the reference program's by a relative error of at most 0.0031.
Values may be sent and summed in bfloat16 or wider, within the bound.
No kernel may reach another device: no remote copies, remote signals or barrier semaphores. Data moves between devices by JAX's collectives and lax.ppermute only.
A program may use at most 128 MiB of HBM per device.

```python
import math
import jax
import jax.numpy as jnp
from jax import lax

BS = 64
NB = 128
NEIGH = 6
REACH = 32
AIR = 64
SWEEPS = 2
SLICES = 8
BLOCKS = 512
AIRT = 256
N_SPACE = 4


def draw_neighbour_cols(key, part):
    first_key = jax.random.fold_in(key, 11)
    second_key = jax.random.fold_in(key, 12)
    third_key = jax.random.fold_in(key, 13)
    block_rows = jnp.arange(BLOCKS, dtype=jnp.int32)
    shuffled = jax.random.permutation(first_key, BLOCKS)
    leading = jnp.where(shuffled < BLOCKS // 2, REACH, -REACH).astype(jnp.int32)
    distances = jax.random.randint(second_key, (NEIGH - 1, BLOCKS), 1, REACH + 1)
    directions = jax.random.randint(third_key, (NEIGH - 1, BLOCKS), 0, 2) * 2 - 1
    displacement = jnp.concatenate([leading[None, :], distances * directions], axis=0)
    return jnp.mod(block_rows[None, :] + displacement, BLOCKS).astype(jnp.int32)


def draw_offsets(key, part):
    first_key = jax.random.fold_in(key, 21)
    second_key = jax.random.fold_in(key, 22)
    drawn = jax.random.randint(first_key, (SLICES,), 0, AIRT)
    shuffled = jax.random.permutation(second_key, SLICES)
    drawn = jnp.where(shuffled == 0, AIRT - 1, jnp.where(shuffled == 1, 0, drawn))
    return drawn.astype(jnp.int32)


def draw_self_blocks(key, part):
    identity = jnp.eye(BS, dtype=jnp.float32)[:, :, None]
    perturb = 0.05 * jax.random.normal(key, (BS, BS, BLOCKS), jnp.float32)
    return 4.0 * identity + perturb


def draw_inverse_blocks(key, part):
    identity = jnp.eye(BS, dtype=jnp.float32)[:, :, None]
    perturb = 0.01 * jax.random.normal(key, (BS, BS, BLOCKS), jnp.float32)
    return 0.2 * identity + perturb


def block_scale(stream_key, dims, pieces, low, top_value):
    def one(position, parts):
        steps = jax.random.uniform(jax.random.fold_in(jax.random.fold_in(stream_key, 6), position), (parts,), jnp.float32, low / len(pieces), top_value / len(pieces))
        return jnp.repeat(jnp.exp(steps), dims[position] // parts).reshape((-1,) + (1,) * (len(dims) - position - 1))

    level = one(*pieces[0])
    for cut in pieces[1:]:
        level = level * one(*cut)
    return level


def normal_values(own_key, extent, scale, limit, cuts=(), held_as=jnp.bfloat16):
    entries = scale * jax.random.normal(own_key, extent, jnp.float32)
    if cuts:
        entries = entries * block_scale(own_key, extent, cuts, -0.22, 0.18)
    return jnp.clip(entries, -limit, limit).astype(held_as)


def setup_inputs(seed: int = 0) -> dict:
    keys = jax.random.split(jax.random.key(seed), 10)
    slice_start = normal_values(keys[0], (SLICES, BS, BLOCKS), 1.0, 6.0, ((0, 8), (2, 4)), jnp.float32)
    conductance = jnp.clip(jnp.exp(math.log(2.0) - 1.3862944 * jax.random.uniform(keys[1], (BS, BLOCKS), jnp.float32) ** block_scale(keys[1], (BS, BLOCKS), ((1, 4),), -0.2, 0.2)), 0.5, 2.0)
    excitation = normal_values(keys[2], (SLICES, 2, BS, BLOCKS), 1.0, 6.0, ((0, 8), (3, 4)), jnp.float32)
    self_blocks = draw_self_blocks(jax.random.fold_in(keys[9], 71), 0)
    coupling = normal_values(keys[4], (NEIGH, BS, BS, BLOCKS), 0.1, 0.59765625, ((3, 4),))
    neighbour_cols = draw_neighbour_cols(jax.random.fold_in(keys[9], 71), 0)
    mortar = normal_values(keys[6], (BS, BS, AIRT), 0.1, 0.59765625, ((2, 4),))
    inverse_blocks = draw_inverse_blocks(jax.random.fold_in(keys[9], 71), 0)
    offsets = draw_offsets(jax.random.fold_in(keys[9], 71), 0)
    return {"slice_start": slice_start, "conductance": conductance, "excitation": excitation, "self_blocks": self_blocks, "coupling": coupling, "neighbour_cols": neighbour_cols, "mortar": mortar, "inverse_blocks": inverse_blocks, "offsets": offsets}


def operate(potential, mass_scale, offset_now, conductance, self_blocks, coupling_wide, neighbour_cols, mortar_wide):
    rounded = potential.astype(jnp.bfloat16)
    nearby = rounded[:, neighbour_cols].astype(jnp.float32)
    product = jnp.einsum("kijr,jkr->ir", coupling_wide, nearby, precision=lax.Precision.HIGHEST)
    product = product + jnp.einsum("ijr,jr->ir", self_blocks, potential, precision=lax.Precision.HIGHEST)
    product = product + mass_scale * conductance * potential
    air_layer = rounded.reshape(BS, N_SPACE, NB)[:, :, :AIR].reshape(BS, AIRT)
    facing = jnp.roll(air_layer, -offset_now, axis=1).astype(jnp.float32)
    mortar_term = jnp.einsum("ijq,jq->iq", mortar_wide, facing, precision=lax.Precision.HIGHEST).reshape(BS, N_SPACE, AIR)
    blocked = product.reshape(BS, N_SPACE, NB)
    blocked = jnp.concatenate([blocked[:, :, :AIR] + mortar_term, blocked[:, :, AIR:]], axis=2)
    return blocked.reshape(BS, BLOCKS)


def advance(potential, source, mass_scale, offset_now, conductance, self_blocks, coupling_wide, neighbour_cols, mortar_wide, inverse_blocks):
    right_side = mass_scale * conductance * potential + source
    iterate = potential
    for sweep_index in range(SWEEPS):
        defect = right_side - operate(iterate, mass_scale, offset_now, conductance, self_blocks, coupling_wide, neighbour_cols, mortar_wide)
        iterate = iterate + jnp.einsum("ijr,jr->ir", inverse_blocks, defect, precision=lax.Precision.HIGHEST)
    return iterate


def reference(slice_start, conductance, excitation, self_blocks, coupling, neighbour_cols, mortar, inverse_blocks, offsets):
    coupling_wide = coupling.astype(jnp.float32)
    mortar_wide = mortar.astype(jnp.float32)
    shared = (conductance, self_blocks, coupling_wide, neighbour_cols, mortar_wide, inverse_blocks)
    fine_ends = []
    coarse_olds = []
    coarse_sources = []
    for slice_index in range(SLICES):
        offset_now = offsets[slice_index]
        beginning = slice_start[slice_index]
        midway = advance(beginning, excitation[slice_index, 0], 1.0, offset_now, *shared)
        fine_ends.append(advance(midway, excitation[slice_index, 1], 1.0, offset_now, *shared))
        coarse_source = 0.5 * (excitation[slice_index, 0] + excitation[slice_index, 1])
        coarse_sources.append(coarse_source)
        coarse_olds.append(advance(beginning, coarse_source, 0.5, offset_now, *shared))
    arrivals = []
    corrections = []
    for slice_index in range(SLICES):
        arrived = fine_ends[(slice_index - 1) % SLICES]
        arrivals.append(arrived)
        coarse_new = advance(arrived, coarse_sources[slice_index], 0.5, offsets[slice_index], *shared)
        corrections.append(coarse_new - coarse_olds[slice_index])
    return (jnp.stack(arrivals), jnp.stack(corrections))
```

```python
import functools

import jax
import jax.numpy as jnp
from jax import lax
from jax.experimental import pallas as pl
from jax.experimental.pallas import tpu as pltpu
from jax.sharding import PartitionSpec as P

REACH = 32
GROUP = 8
VMEM = pltpu.MemorySpace.VMEM
SMEM = pltpu.MemorySpace.SMEM


def pairing(count):
    return (count & (count - 1)) == 0


def partner(position, slot, count):
    if pairing(count):
        return position ^ slot
    return (position + slot) % count


def slot_of(position, device, count):
    if pairing(count):
        return position ^ device
    return lax.rem(position - device + count, count)


def exchange(block, count):
    return [
        lax.ppermute(block, "space", [(i, partner(i, k, count)) for i in range(count)])
        for k in range(1, count)
    ]


def exchange_next(exact, rounded, count, slices):
    def moved(block, slot):
        pairs = [
            (t * count + i, ((t + 1) % slices) * count + partner(i, slot, count))
            for t in range(slices)
            for i in range(count)
        ]
        return lax.ppermute(block, ("tm", "space"), pairs)

    return moved(exact, 0), [moved(rounded, k) for k in range(1, count)]


def widen_kernel(coupling_ref, mortar_ref, wide_ref):
    near, air = coupling_ref.shape[0], mortar_ref.shape[2]
    start = pl.multiple_of(pl.program_id(0) * GROUP, GROUP)
    for k in range(near):
        wide_ref[pl.ds(start, GROUP), k] = coupling_ref[k].astype(jnp.float32)
    face = mortar_ref[...].astype(jnp.float32)
    rest = wide_ref.shape[3] - air
    wide_ref[pl.ds(start, GROUP), near] = jnp.concatenate(
        [face, jnp.zeros(face.shape[:2] + (rest,), jnp.float32)], axis=2
    )


def widen(coupling, mortar):
    near, edges, _, blocks = coupling.shape
    air = mortar.shape[2]
    shape = (edges, near + 1, edges, blocks)
    return pl.pallas_call(
        widen_kernel,
        grid=(edges // GROUP,),
        in_specs=[
            pl.BlockSpec((near, GROUP, edges, blocks), lambda g: (0, g, 0, 0)),
            pl.BlockSpec((GROUP, edges, air), lambda g: (g, 0, 0)),
        ],
        out_specs=pl.BlockSpec(memory_space=VMEM),
        out_shape=pltpu.VMEM(shape, jnp.float32),
        compiler_params=pltpu.CompilerParams(vmem_limit_bytes=24 << 20),
        cost_estimate=pl.CostEstimate(flops=0, bytes_accessed=8 << 20, transcendentals=0),
    )(coupling, mortar)


def rounded_wide(x):
    return x.astype(jnp.bfloat16).astype(jnp.float32)


def sweep_kernel(stage, count, *refs):
    (off_ref, cols_ref, wide_ref, self_ref, inv_ref, cond_ref) = refs[:6]
    refs = refs[6:]
    edges, blocks = cond_ref.shape
    near = cols_ref.shape[0]
    air = blocks // 2
    conductance = cond_ref[...]
    if stage == "first":
        start_ref, source_ref = refs[:2]
        refs = refs[2:]
        x = start_ref[...]
        rhs = conductance * x + source_ref[...]
    elif stage == "second":
        x_ref, start_ref, source_ref = refs[:3]
        refs = refs[3:]
        x = x_ref[...]
        rhs = conductance * start_ref[...] + source_ref[...]
    else:
        if stage == "fourth":
            x_ref = refs[0]
            refs = refs[1:]
        new_ref, old_ref, first_ref, last_ref = refs[:4]
        refs = refs[4:]
        new, old = new_ref[...], old_ref[...]
        source = 0.5 * (first_ref[...] + last_ref[...])
        half = 0.5 * conductance
        rhs = (half * new + source) - (half * old + source)
        x = new - old if stage == "third" else x_ref[...]
    scale = 0.5 if stage in ("third", "fourth") else 1.0

    messages = refs[: count - 1]
    refs = refs[count - 1 :]
    if stage == "third":
        before = refs[: count - 1]
        refs = refs[count - 1 :]
    out_ref, out_rounded_ref = refs[:2]
    table_ref, near_ref, defect_ref = refs[2:]

    if stage == "third":
        table_ref[0] = rounded_wide(new) - rounded_wide(old)
    else:
        table_ref[0] = rounded_wide(x)
    for k in range(1, count):
        got = messages[k - 1][...].astype(jnp.float32)
        if stage == "third":
            got = got - before[k - 1][...].astype(jnp.float32)
        table_ref[k] = got

    position = lax.axis_index("space")
    after = lax.rem(position + 1, count)
    ahead = lax.rem(position + count - 1, count)
    lane = lax.broadcasted_iota(jnp.int32, (edges, blocks), 1)
    own = table_ref[0]
    beside = jnp.where(
        lane < air,
        table_ref[slot_of(position, after, count)],
        table_ref[slot_of(position, ahead, count)],
    )
    for k in range(near):
        column = jnp.broadcast_to(cols_ref[k : k + 1, :], (edges, blocks))
        place = lax.rem(column, blocks)
        inside = column - place == position * blocks
        near_ref[k] = jnp.where(
            inside,
            jnp.take_along_axis(own, place, axis=1),
            jnp.take_along_axis(beside, place, axis=1),
        )
    turn = off_ref[0]
    low = lax.rem(position + lax.div(turn, air), count)
    high = lax.rem(low + 1, count)
    shift = lax.rem(turn, air)
    layer = jnp.where(
        lane < air,
        table_ref[slot_of(position, low, count)],
        pltpu.roll(table_ref[slot_of(position, high, count)], air, 1),
    )
    facing = pltpu.roll(layer, lax.rem(blocks - shift, blocks), 1)
    near_ref[near] = jnp.where(lane < air, facing, 0.0)

    near_ref[near + 1] = x
    tiles = edges // 8

    def product(matrix, vector):
        split = matrix.reshape(GROUP, tiles, 8, blocks)
        return jnp.sum(split * vector.reshape(1, tiles, 8, blocks), axis=1)

    def defect_rows(g, carry):
        rows = pl.ds(pl.multiple_of(g * GROUP, GROUP), GROUP)
        total = product(self_ref[rows], near_ref[near + 1])
        for k in range(near + 1):
            total = total + product(wide_ref[rows, k], near_ref[k])
        defect_ref[rows, :] = jnp.sum(total, axis=1)
        return carry

    lax.fori_loop(0, edges // GROUP, defect_rows, 0)
    near_ref[0] = rhs - (defect_ref[...] + scale * conductance * x)

    def update_rows(g, carry):
        rows = pl.ds(pl.multiple_of(g * GROUP, GROUP), GROUP)
        defect_ref[rows, :] = jnp.sum(product(inv_ref[rows], near_ref[0]), axis=1)
        return carry

    lax.fori_loop(0, edges // GROUP, update_rows, 0)
    result = x + defect_ref[...]
    out_ref[...] = result
    out_rounded_ref[...] = result.astype(jnp.bfloat16)


def sweep(stage, count, shared, state, messages, before=()):
    offsets, cols, wide, self_blocks, inverse, conductance = shared
    edges, blocks = conductance.shape
    near = cols.shape[0]
    wide, self_blocks, inverse = (
        pltpu.with_memory_space_constraint(a, VMEM) for a in (wide, self_blocks, inverse)
    )
    operands = [offsets, cols, wide, self_blocks, inverse, conductance, *state, *messages, *before]
    specs = [pl.BlockSpec(memory_space=SMEM)]
    specs += [pl.BlockSpec(memory_space=VMEM)] * (len(operands) - 1)
    return pl.pallas_call(
        functools.partial(sweep_kernel, stage, count),
        in_specs=specs,
        out_specs=[pl.BlockSpec(memory_space=VMEM)] * 2,
        out_shape=[
            jax.ShapeDtypeStruct((edges, blocks), jnp.float32),
            jax.ShapeDtypeStruct((edges, blocks), jnp.bfloat16),
        ],
        scratch_shapes=[
            pltpu.VMEM((count, edges, blocks), jnp.float32),
            pltpu.VMEM((near + 2, edges, blocks), jnp.float32),
            pltpu.VMEM((edges, blocks), jnp.float32),
        ],
        compiler_params=pltpu.CompilerParams(vmem_limit_bytes=16 << 20),
        cost_estimate=pl.CostEstimate(
            flops=2 * edges * edges * blocks * (near + 3), bytes_accessed=1 << 20, transcendentals=0
        ),
    )(*operands)


def per_device(
    slice_start,
    conductance,
    excitation,
    self_blocks,
    coupling,
    neighbour_cols,
    mortar,
    inverse_blocks,
    offsets,
):
    count = lax.axis_size("space")
    slices = lax.axis_size("tm")
    start = slice_start[0]
    first, last = excitation[0, 0], excitation[0, 1]
    start_near = exchange(start.astype(jnp.bfloat16), count)
    wide = widen(coupling, mortar)
    shared = (offsets, neighbour_cols, wide, self_blocks, inverse_blocks, conductance)

    x, r = sweep("first", count, shared, (start, first), start_near)
    midway, r = sweep("second", count, shared, (x, start, first), exchange(r, count))
    x, r = sweep("first", count, shared, (midway, last), exchange(r, count))
    fine, r = sweep("second", count, shared, (x, midway, last), exchange(r, count))
    arrived, arrived_near = exchange_next(fine, r, count, slices)
    ends = (arrived, start, first, last)
    x, r = sweep("third", count, shared, ends, arrived_near, start_near)
    correction, _ = sweep("fourth", count, shared, (x, *ends), exchange(r, count))
    return (arrived[None], correction[None])


def solution(mesh):
    in_specs = (
        P("tm", None, "space"),
        P(None, "space"),
        P("tm", None, None, "space"),
        P(None, None, "space"),
        P(None, None, None, "space"),
        P(None, "space"),
        P(None, None, "space"),
        P(None, None, "space"),
        P("tm"),
    )
    out_specs = (P("tm", None, "space"), P("tm", None, "space"))
    return jax.shard_map(
        per_device, mesh=mesh, in_specs=in_specs, out_specs=out_specs, check_vma=False
    )
```

```python
import functools

import jax
import jax.numpy as jnp
from jax import lax
from jax.experimental import pallas as pl
from jax.experimental.pallas import tpu as pltpu
from jax.sharding import PartitionSpec as P

REACH = 32
SUBLANES = 8
GROUP = 8
VMEM = pltpu.MemorySpace.VMEM
SMEM = pltpu.MemorySpace.SMEM
MIB = 1 << 20


def pairing(count):
    return (count & (count - 1)) == 0


def partner(position, slot, count):
    if pairing(count):
        return position ^ slot
    return (position + slot) % count


def slot_of(position, device, count):
    if pairing(count):
        return position ^ device
    return lax.rem(position - device + count, count)


def exchange(block, count):
    return [
        lax.ppermute(block, "space", [(i, partner(i, k, count)) for i in range(count)])
        for k in range(1, count)
    ]


def exchange_next(exact, rounded, count, slices):
    def moved(block, slot):
        pairs = [
            (t * count + i, ((t + 1) % slices) * count + partner(i, slot, count))
            for t in range(slices)
            for i in range(count)
        ]
        return lax.ppermute(block, ("tm", "space"), pairs)

    return moved(exact, 0), [moved(rounded, k) for k in range(1, count)]


def call(body, operands, outputs, scratch=(), limit=8, flops=0, in_specs=None):
    return pl.pallas_call(
        body,
        in_specs=in_specs or [pl.BlockSpec(memory_space=VMEM)] * len(operands),
        out_specs=[pl.BlockSpec(memory_space=VMEM)] * len(outputs),
        out_shape=outputs,
        scratch_shapes=list(scratch),
        compiler_params=pltpu.CompilerParams(vmem_limit_bytes=limit * MIB),
        cost_estimate=pl.CostEstimate(flops=flops, bytes_accessed=MIB, transcendentals=0),
    )(*operands)


def lanes(shape):
    return lax.broadcasted_iota(jnp.int32, shape, len(shape) - 1)


def outer_lanes(shape):
    lane = lanes(shape)
    return (lane < REACH) | (lane >= shape[-1] - REACH)


def round_kernel(start_ref, rounded_ref):
    rounded_ref[...] = start_ref[0].astype(jnp.bfloat16)


def pack_kernel(coupling_ref, mortar_ref, packed_ref, face_ref):
    near, edges, _, blocks = coupling_ref.shape
    half, air = near // 2, mortar_ref.shape[2]
    outer = outer_lanes((edges, blocks))

    def row(i, carry):
        for k in range(half):
            one = coupling_ref[k, i].astype(jnp.float32)
            other = coupling_ref[k + half, i].astype(jnp.float32)
            packed_ref[i, k] = jnp.where(outer, one, pltpu.roll(other, blocks // 2, 1))
        face = mortar_ref[i].astype(jnp.float32)
        face_ref[i] = jnp.concatenate([face[: edges // 2], face[edges // 2 :]], axis=1)
        return carry

    lax.fori_loop(0, edges, row, 0)


def pack(coupling, mortar):
    near, edges, _, blocks = coupling.shape
    operands = [pltpu.with_memory_space_constraint(a, VMEM) for a in (coupling, mortar)]
    outputs = [
        pltpu.VMEM((edges, near // 2, edges, blocks), jnp.float32),
        pltpu.VMEM((edges, edges // 2, blocks), jnp.float32),
    ]
    return call(pack_kernel, operands, outputs, limit=2)


def rounded_wide(x):
    return x.astype(jnp.bfloat16).astype(jnp.float32)


def rows_of(g):
    return pl.ds(pl.multiple_of(g * GROUP, GROUP), GROUP)


def product(matrix, vector):
    depth, blocks = vector.shape
    tiles = depth // SUBLANES
    split = matrix.astype(jnp.float32).reshape(GROUP, tiles, SUBLANES, blocks)
    return jnp.sum(split * vector.reshape(1, tiles, SUBLANES, blocks), axis=1)


def column_places(cols_ref, k, shape, position):
    column = jnp.broadcast_to(cols_ref[k : k + 1, :], shape)
    place = column & (shape[1] - 1)
    return place, column - place == position * shape[1]


def local_body(stage, step, *refs):
    cols_ref, coupling_ref, self_ref, cond_ref, source_ref = refs[:5]
    near_ref, sums_ref = refs[-2:]
    refs = refs[5:-2]
    edges, blocks = cond_ref.shape
    near = cols_ref.shape[0]
    conductance = cond_ref[...]
    if stage in ("third", "fourth"):
        new, old = refs[0][...], refs[1][0]
        source = 0.5 * (source_ref[0, 0] + source_ref[0, 1])
        half = 0.5 * conductance
        rhs = (half * new + source) - (half * old + source)
        scale = 0.5
        if stage == "third":
            x = new - old
            own = rounded_wide(new) - rounded_wide(old)
            part_ref = refs[2]
        else:
            x = refs[2][...]
            own = rounded_wide(x)
            part_ref, arrived_ref = refs[3:]
            arrived_ref[0] = new
    else:
        source = source_ref[0, step]
        base = refs[0][...]
        base = base[0] if base.ndim == 3 else base
        x = base if stage == "first" else refs[1][...]
        rhs = conductance * base + source
        scale = 1.0
        own = rounded_wide(x)
        part_ref = refs[-1]

    position = lax.axis_index("space")
    near_ref[near] = x
    for k in range(near):
        place, inside = column_places(cols_ref, k, (edges, blocks), position)
        near_ref[k] = jnp.where(inside, jnp.take_along_axis(own, place, axis=1), 0.0)

    def rows(g, carry):
        here = rows_of(g)
        total = product(self_ref[here], near_ref[near])
        for k in range(near):
            total = total + product(coupling_ref[k, here], near_ref[k])
        sums_ref[here, :] = jnp.sum(total, axis=1)
        return carry

    lax.fori_loop(0, edges // GROUP, rows, 0)
    part_ref[...] = rhs - (sums_ref[...] + scale * conductance * x)


def remote_body(stage, count, off_ref, cols_ref, packed_ref, face_ref, inv_ref, part_ref, *refs):
    table_ref, near_ref, layer_ref, sums_ref = refs[-4:]
    refs = refs[:-4]
    edges, blocks = part_ref.shape
    near = cols_ref.shape[0]
    half, air = near // 2, blocks // 2
    messages, refs = refs[:count], refs[count:]
    if stage == "third":
        before, refs = refs[:count], refs[count:]
        new_ref, old_ref, out_ref, rounded_ref = refs
        x = new_ref[...] - old_ref[0]
    else:
        x_ref, out_ref, rounded_ref = refs
        x = x_ref[...]
        x = x[0] if x.ndim == 3 else x
    for k in range(count):
        got = messages[k][...].astype(jnp.float32)
        if stage == "third":
            got = got - before[k][...].astype(jnp.float32)
        table_ref[k] = got

    position = lax.axis_index("space")
    after = lax.rem(position + 1, count)
    ahead = lax.rem(position + count - 1, count)
    lane = lanes((edges, blocks))
    outer = outer_lanes((edges, blocks))
    beside = jnp.where(
        lane < air,
        table_ref[slot_of(position, after, count)],
        table_ref[slot_of(position, ahead, count)],
    )

    def reached(k):
        place, inside = column_places(cols_ref, k, (edges, blocks), position)
        return jnp.where(inside, 0.0, jnp.take_along_axis(beside, place, axis=1))

    for k in range(half):
        near_ref[k] = jnp.where(outer, reached(k), pltpu.roll(reached(k + half), blocks // 2, 1))

    turn = off_ref[0]
    low = lax.rem(position + lax.div(turn, air), count)
    high = lax.rem(low + 1, count)
    shift = lax.rem(turn, air)
    layer = jnp.where(
        lane < air,
        table_ref[slot_of(position, low, count)],
        pltpu.roll(table_ref[slot_of(position, high, count)], air, 1),
    )
    facing = pltpu.roll(layer, lax.rem(blocks - shift, blocks), 1)
    deep = edges // 2
    layer_ref[...] = jnp.where(
        lanes((deep, blocks)) < air, facing[:deep], pltpu.roll(facing[deep:], air, 1)
    )

    def rows(g, carry):
        here = rows_of(g)
        total = product(packed_ref[here, 0], near_ref[0])
        for k in range(1, half):
            total = total + product(packed_ref[here, k], near_ref[k])
        far = jnp.sum(total, axis=1)
        face = jnp.sum(product(face_ref[here], layer_ref[...]), axis=1)
        out = outer_lanes(far.shape)
        folded = far + pltpu.roll(far, blocks // 2, 1)
        faced = face + pltpu.roll(face, air, 1)
        sums_ref[here, :] = jnp.where(out, folded, 0.0) + jnp.where(
            lanes(face.shape) < air, faced, 0.0
        )
        return carry

    lax.fori_loop(0, edges // GROUP, rows, 0)
    near_ref[0] = part_ref[...] - sums_ref[...]

    def update(g, carry):
        here = rows_of(g)
        sums_ref[here, :] = jnp.sum(product(inv_ref[here], near_ref[0]), axis=1)
        return carry

    lax.fori_loop(0, edges // GROUP, update, 0)
    result = x + sums_ref[...]
    if stage == "last":
        out_ref[0] = result
    else:
        out_ref[...] = result
        rounded_ref[...] = result.astype(jnp.bfloat16)


def per_device(
    slice_start,
    conductance,
    excitation,
    self_blocks,
    coupling,
    neighbour_cols,
    mortar,
    inverse_blocks,
    offsets,
):
    count = lax.axis_size("space")
    slices = lax.axis_size("tm")
    near, edges, _, blocks = coupling.shape
    field = jax.ShapeDtypeStruct((edges, blocks), jnp.float32)
    short = jax.ShapeDtypeStruct((edges, blocks), jnp.bfloat16)
    whole = jax.ShapeDtypeStruct((1, edges, blocks), jnp.float32)
    keep = functools.partial(pltpu.with_memory_space_constraint, memory_space=VMEM)
    work = 2 * edges * edges * blocks

    (rounded,) = call(round_kernel, [slice_start], [short], flops=1 << 36, limit=1)
    start_near = exchange(rounded, count)
    packed, face = pack(coupling, mortar)

    def local(stage, step, state, outputs=()):
        operands = [neighbour_cols, keep(coupling), keep(self_blocks), conductance, excitation, *state]
        scratch = [
            pltpu.VMEM((near + 1, edges, blocks), jnp.float32),
            pltpu.VMEM((edges, blocks), jnp.float32),
        ]
        body = functools.partial(local_body, stage, step)
        return call(body, operands, [field, *outputs], scratch, flops=work * near)

    def remote(stage, part, messages, state):
        operands = [
            offsets, neighbour_cols, keep(packed), keep(face), keep(inverse_blocks), part,
            *messages, *state,
        ]
        specs = [pl.BlockSpec(memory_space=SMEM)]
        specs += [pl.BlockSpec(memory_space=VMEM)] * (len(operands) - 1)
        scratch = [
            pltpu.VMEM((count, edges, blocks), jnp.float32),
            pltpu.VMEM((near // 2, edges, blocks), jnp.float32),
            pltpu.VMEM((edges // 2, blocks), jnp.float32),
            pltpu.VMEM((edges, blocks), jnp.float32),
        ]
        outputs = [whole] if stage == "last" else [field, short]
        body = functools.partial(remote_body, stage, count)
        if stage == "last":
            body = lambda *refs: remote_body(stage, count, *refs[:-4], None, *refs[-4:])
        return call(body, operands, outputs, scratch, flops=work * near, in_specs=specs)

    start_table = [rounded, *start_near]
    (part,) = local("first", 0, [slice_start])
    x, r = remote("plain", part, start_table, [slice_start])
    got = exchange(r, count)
    (part,) = local("second", 0, [slice_start, x])
    midway, r = remote("plain", part, [r, *got], [x])
    got = exchange(r, count)
    (part,) = local("first", 1, [midway])
    x, r = remote("plain", part, [r, *got], [midway])
    got = exchange(r, count)
    (part,) = local("second", 1, [midway, x])
    fine, r = remote("plain", part, [r, *got], [x])

    arrived, got = exchange_next(fine, r, count, slices)
    (part,) = local("third", 0, [arrived, slice_start])
    arrived_short = arrived.astype(jnp.bfloat16)
    x, r = remote(
        "third", part, [arrived_short, *got], [*start_table, arrived, slice_start]
    )
    got = exchange(r, count)
    part, new_start = local("fourth", 0, [arrived, slice_start, x], [whole])
    (correction,) = remote("last", part, [r, *got], [x])
    return (new_start, correction)


def solution(mesh):
    in_specs = (
        P("tm", None, "space"),
        P(None, "space"),
        P("tm", None, None, "space"),
        P(None, None, "space"),
        P(None, None, None, "space"),
        P(None, "space"),
        P(None, None, "space"),
        P(None, None, "space"),
        P("tm"),
    )
    out_specs = (P("tm", None, "space"), P("tm", None, "space"))
    return jax.shard_map(
        per_device, mesh=mesh, in_specs=in_specs, out_specs=out_specs, check_vma=False
    )
```

```python
import functools

import jax
import jax.numpy as jnp
from jax import lax
from jax.experimental import pallas as pl
from jax.experimental.pallas import tpu as pltpu
from jax.sharding import PartitionSpec as P

REACH = 32
SUBLANES = 8
PACK = 8
LOCAL_GROUP = 16
REMOTE_GROUP = 16
UPDATE_GROUP = 32
VMEM = pltpu.MemorySpace.VMEM
SMEM = pltpu.MemorySpace.SMEM
MIB = 1 << 20


def pairing(count):
    return (count & (count - 1)) == 0


def partner(position, slot, count):
    if pairing(count):
        return position ^ slot
    return (position + slot) % count


def slot_of(position, device, count):
    if pairing(count):
        return position ^ device
    return lax.rem(position - device + count, count)


def exchange(block, count):
    return [
        lax.ppermute(block, "space", [(i, partner(i, k, count)) for i in range(count)])
        for k in range(1, count)
    ]


def exchange_next(exact, rounded, count, slices):
    def moved(block, slot):
        pairs = [
            (t * count + i, ((t + 1) % slices) * count + partner(i, slot, count))
            for t in range(slices)
            for i in range(count)
        ]
        return lax.ppermute(block, ("tm", "space"), pairs)

    return moved(exact, 0), [moved(rounded, k) for k in range(1, count)]


def call(body, operands, outputs, scratch=(), limit=8, flops=0, in_specs=None):
    return pl.pallas_call(
        body,
        in_specs=in_specs or [pl.BlockSpec(memory_space=VMEM)] * len(operands),
        out_specs=[pl.BlockSpec(memory_space=VMEM)] * len(outputs),
        out_shape=outputs,
        scratch_shapes=list(scratch),
        compiler_params=pltpu.CompilerParams(vmem_limit_bytes=limit * MIB),
        cost_estimate=pl.CostEstimate(flops=flops, bytes_accessed=MIB, transcendentals=0),
    )(*operands)


def lanes(shape):
    return lax.broadcasted_iota(jnp.int32, shape, len(shape) - 1)


def outer_lanes(shape):
    lane = lanes(shape)
    return (lane < REACH) | (lane >= shape[-1] - REACH)


def round_kernel(start_ref, rounded_ref):
    rounded_ref[...] = start_ref[0].astype(jnp.bfloat16)


def place_of(cols_ref, k, position, shape):
    blocks = shape[1]
    column = jnp.broadcast_to(cols_ref[k : k + 1, :], shape)
    place = column & (blocks - 1)
    return place, column - place == position * blocks


def pack_kernel(coupling_ref, mortar_ref, cols_ref, packed_ref, face_ref, places_ref):
    near, edges, _, blocks = coupling_ref.shape
    half, middle = near // 2, blocks // 2
    outer = outer_lanes((edges, blocks))
    position = lax.axis_index("space")
    thin = (SUBLANES, blocks)
    for k in range(half):
        wanted = []
        for kk in (k, k + half):
            place, inside = place_of(cols_ref, kk, position, thin)
            wanted.append(jnp.where(inside, -1, place))
        places_ref[k] = jnp.where(outer_lanes(thin), wanted[0], pltpu.roll(wanted[1], middle, 1))

    def rows(g, carry):
        for step in range(PACK):
            i = g * PACK + step
            for k in range(half):
                one = coupling_ref[k, i].astype(jnp.float32)
                other = coupling_ref[k + half, i].astype(jnp.float32)
                packed_ref[i, k] = jnp.where(outer, one, pltpu.roll(other, middle, 1))
            face = mortar_ref[i].astype(jnp.float32)
            face_ref[i] = jnp.concatenate([face[: edges // 2], face[edges // 2 :]], axis=1)
        return carry

    lax.fori_loop(0, edges // PACK, rows, 0)


def pack(coupling, mortar, cols):
    near, edges, _, blocks = coupling.shape
    operands = [pltpu.with_memory_space_constraint(a, VMEM) for a in (coupling, mortar)]
    outputs = [
        pltpu.VMEM((edges, near // 2, edges, blocks), jnp.float32),
        pltpu.VMEM((edges, edges // 2, blocks), jnp.float32),
        jax.ShapeDtypeStruct((near // 2, SUBLANES, blocks), jnp.int32),
    ]
    return call(pack_kernel, [*operands, cols], outputs, limit=2)


def rounded_wide(x):
    return x.astype(jnp.bfloat16).astype(jnp.float32)


def product(matrix, vector):
    depth, blocks = vector.shape
    tiles = depth // SUBLANES
    split = matrix.astype(jnp.float32).reshape(-1, tiles, SUBLANES, blocks)
    return jnp.sum(split * vector.reshape(1, tiles, SUBLANES, blocks), axis=1)


def sweep_rows(edges, group, partial):
    def step(g, carry):
        partial(pl.ds(pl.multiple_of(g * group, group), group))
        return carry

    lax.fori_loop(0, edges // group, step, 0)


def local_body(stage, step, *refs):
    cols_ref, coupling_ref, self_ref, cond_ref, source_ref = refs[:5]
    near_ref, sums_ref = refs[-2:]
    refs = refs[5:-2]
    edges, blocks = cond_ref.shape
    near = cols_ref.shape[0]
    conductance = cond_ref[...]
    if stage in ("third", "fourth"):
        new, old = refs[0][...], refs[1][0]
        source = 0.5 * (source_ref[0, 0] + source_ref[0, 1])
        half = 0.5 * conductance
        rhs = (half * new + source) - (half * old + source)
        scale = 0.5
        if stage == "third":
            x = new - old
            own = rounded_wide(new) - rounded_wide(old)
            part_ref = refs[2]
        else:
            x = refs[2][...]
            own = rounded_wide(x)
            part_ref, arrived_ref = refs[3:]
            arrived_ref[0] = new
    else:
        source = source_ref[0, step]
        base = refs[0][...]
        base = base[0] if base.ndim == 3 else base
        x = base if stage == "first" else refs[1][...]
        rhs = conductance * base + source
        scale = 1.0
        own = rounded_wide(x)
        part_ref = refs[-1]
    part_ref[...] = rhs - scale * conductance * x

    position = lax.axis_index("space")
    near_ref[near] = x
    for k in range(near):
        place, inside = place_of(cols_ref, k, position, (edges, blocks))
        near_ref[k] = jnp.where(inside, jnp.take_along_axis(own, place, axis=1), 0.0)

    def partial(here):
        total = product(self_ref[here], near_ref[near])
        for k in range(near):
            total = total + product(coupling_ref[k, here], near_ref[k])
        sums_ref[here] = total

    sweep_rows(edges, LOCAL_GROUP, partial)
    part_ref[...] = part_ref[...] - jnp.sum(sums_ref[...], axis=1)


def remote_body(
    stage, count, off_ref, places_ref, packed_ref, face_ref, inv_ref, part_ref, *refs
):
    table_ref, near_ref, layer_ref, sums_ref, faces_ref = refs[-5:]
    refs = refs[:-5]
    edges, blocks = part_ref.shape
    half, air, deep = places_ref.shape[0], blocks // 2, edges // 2
    messages, refs = refs[:count], refs[count:]
    if stage == "third":
        before, refs = refs[:count], refs[count:]
        new_ref, old_ref, out_ref, rounded_ref = refs
        x = new_ref[...] - old_ref[0]
    else:
        x_ref, out_ref, rounded_ref = refs
        x = x_ref[...]
        x = x[0] if x.ndim == 3 else x
    for k in range(count):
        got = messages[k][...].astype(jnp.float32)
        if stage == "third":
            got = got - before[k][...].astype(jnp.float32)
        table_ref[k] = got

    position = lax.axis_index("space")
    after = lax.rem(position + 1, count)
    ahead = lax.rem(position + count - 1, count)
    lane = lanes((edges, blocks))
    beside = jnp.where(
        lane < air,
        table_ref[slot_of(position, after, count)],
        table_ref[slot_of(position, ahead, count)],
    )
    for k in range(half):
        place = jnp.broadcast_to(places_ref[k, 0:1], (edges, blocks))
        taken = jnp.take_along_axis(beside, jnp.maximum(place, 0), axis=1)
        near_ref[k] = jnp.where(place >= 0, taken, 0.0)

    turn = off_ref[0]
    low = lax.rem(position + lax.div(turn, air), count)
    high = lax.rem(low + 1, count)
    reach = (lane & (air - 1)) + lax.rem(turn, air)
    place = reach & (air - 1)
    facing = jnp.where(
        reach < air,
        jnp.take_along_axis(table_ref[slot_of(position, low, count)], place, axis=1),
        jnp.take_along_axis(table_ref[slot_of(position, high, count)], place, axis=1),
    )
    layer_ref[...] = jnp.where(lane[:deep] < air, facing[:deep], facing[deep:])

    def partial(here):
        total = product(packed_ref[here, 0], near_ref[0])
        for k in range(1, half):
            total = total + product(packed_ref[here, k], near_ref[k])
        sums_ref[here] = total
        faces_ref[here] = product(face_ref[here], layer_ref[...])

    sweep_rows(edges, REMOTE_GROUP, partial)
    far = jnp.sum(sums_ref[...], axis=1)
    face = jnp.sum(faces_ref[...], axis=1)
    far = jnp.where(outer_lanes(far.shape), far + pltpu.roll(far, blocks // 2, 1), 0.0)
    face = jnp.where(lane < air, face + pltpu.roll(face, air, 1), 0.0)
    near_ref[0] = part_ref[...] - (far + face)

    def update(here):
        sums_ref[here] = product(inv_ref[here], near_ref[0])

    sweep_rows(edges, UPDATE_GROUP, update)
    result = x + jnp.sum(sums_ref[...], axis=1)
    if stage == "last":
        out_ref[0] = result
    else:
        out_ref[...] = result
        rounded_ref[...] = result.astype(jnp.bfloat16)


def per_device(
    slice_start,
    conductance,
    excitation,
    self_blocks,
    coupling,
    neighbour_cols,
    mortar,
    inverse_blocks,
    offsets,
):
    count = lax.axis_size("space")
    slices = lax.axis_size("tm")
    near, edges, _, blocks = coupling.shape
    field = jax.ShapeDtypeStruct((edges, blocks), jnp.float32)
    short = jax.ShapeDtypeStruct((edges, blocks), jnp.bfloat16)
    whole = jax.ShapeDtypeStruct((1, edges, blocks), jnp.float32)
    keep = functools.partial(pltpu.with_memory_space_constraint, memory_space=VMEM)
    work = 2 * edges * edges * blocks

    (rounded,) = call(round_kernel, [slice_start], [short], flops=1 << 36, limit=1)
    start_near = exchange(rounded, count)
    packed, face, places = pack(coupling, mortar, neighbour_cols)

    def local(stage, step, state, outputs=()):
        operands = [neighbour_cols, keep(coupling), keep(self_blocks), conductance, excitation, *state]
        scratch = [
            pltpu.VMEM((near + 1, edges, blocks), jnp.float32),
            pltpu.VMEM((edges, SUBLANES, blocks), jnp.float32),
        ]
        body = functools.partial(local_body, stage, step)
        return call(body, operands, [field, *outputs], scratch, flops=work * near)

    def remote(stage, part, messages, state):
        operands = [
            offsets, places, keep(packed), keep(face), keep(inverse_blocks), part,
            *messages, *state,
        ]
        specs = [pl.BlockSpec(memory_space=SMEM)]
        specs += [pl.BlockSpec(memory_space=VMEM)] * (len(operands) - 1)
        scratch = [
            pltpu.VMEM((count, edges, blocks), jnp.float32),
            pltpu.VMEM((near // 2, edges, blocks), jnp.float32),
            pltpu.VMEM((edges // 2, blocks), jnp.float32),
            pltpu.VMEM((edges, SUBLANES, blocks), jnp.float32),
            pltpu.VMEM((edges, SUBLANES, blocks), jnp.float32),
        ]
        outputs = [whole] if stage == "last" else [field, short]
        body = functools.partial(remote_body, stage, count)
        if stage == "last":
            body = lambda *refs: remote_body(stage, count, *refs[:-5], None, *refs[-5:])
        return call(body, operands, outputs, scratch, flops=work * near, in_specs=specs)

    start_table = [rounded, *start_near]
    (part,) = local("first", 0, [slice_start])
    x, r = remote("plain", part, start_table, [slice_start])
    got = exchange(r, count)
    (part,) = local("second", 0, [slice_start, x])
    midway, r = remote("plain", part, [r, *got], [x])
    got = exchange(r, count)
    (part,) = local("first", 1, [midway])
    x, r = remote("plain", part, [r, *got], [midway])
    got = exchange(r, count)
    (part,) = local("second", 1, [midway, x])
    fine, r = remote("plain", part, [r, *got], [x])

    arrived, got = exchange_next(fine, r, count, slices)
    (part,) = local("third", 0, [arrived, slice_start])
    arrived_short = arrived.astype(jnp.bfloat16)
    x, r = remote(
        "third", part, [arrived_short, *got], [*start_table, arrived, slice_start]
    )
    got = exchange(r, count)
    part, new_start = local("fourth", 0, [arrived, slice_start, x], [whole])
    (correction,) = remote("last", part, [r, *got], [x])
    return (new_start, correction)


def solution(mesh):
    in_specs = (
        P("tm", None, "space"),
        P(None, "space"),
        P("tm", None, None, "space"),
        P(None, None, "space"),
        P(None, None, None, "space"),
        P(None, "space"),
        P(None, None, "space"),
        P(None, None, "space"),
        P("tm"),
    )
    out_specs = (P("tm", None, "space"), P("tm", None, "space"))
    return jax.shard_map(
        per_device, mesh=mesh, in_specs=in_specs, out_specs=out_specs, check_vma=False
    )
```
